256 devices in a mesh: dp: 32 (over y, z), order: 8 (over x, core).
Axes of the slice: x: 4, y: 4, z: 8, core: 2. Of those that a mesh axis runs over, the one named last changes fastest.
Arguments:
- images: bfloat16 [8192, 128, 512], P(('dp', 'order')), may hold values from -6 to 6
- radial_interp: bfloat16 [128, 128], replicated, may hold values from -0.5 to 0.5
- assignment: int32 [256], replicated, may hold values from 0 to 255, as said below
- counts: int32 [256], P('order'), may hold values from 32 to 128, as said below
- radial_basis: bfloat16 [256, 128, 128], P('order'), may hold values from -0.5 to 0.5
- eigenbasis: bfloat16 [256, 128, 128], P('order'), may hold values from -0.5 to 0.5
Outputs:
- covariance: float32 [256, 32768], P(('order', 'dp'))
- projected: bfloat16 [2, 256, 8192, 128], P(None, 'order', 'dp')
The draws below stay inside these ranges and needn't reach their ends.
Inputs may be any that keep to these rules, and one draw needn't show every extreme that they name: `assignment`: a permutation of the orders 0 to 255. The slot of order 0 keeps 128; the slot of order 256 - 1 keeps 32; counts fall with the order up to a jitter of 3.
All inputs are finite; a program needn't handle non-finite values.
Results may differ from the reference program's by a relative error of at most 0.013.
Values may be sent and summed in bfloat16 or wider, within the bound.
No kernel may reach another device: no remote copies, remote signals or barrier semaphores. Data moves between devices by JAX's collectives and lax.ppermute only.
A program may use at most 128 MiB of HBM per device.

```python
import math
import jax
import jax.numpy as jnp
from jax import lax

NA = 512
NR0 = 128
NR = 128
NK = 128
NE = 128
IMG_DEV = 32
ORDERS = 256
NK_MIN = 32
IMAGES = 8192
N_ORDER = 8


def shared_order(key):
    return jax.random.permutation(jax.random.fold_in(key, 7), ORDERS).astype(jnp.int32)


def draw_assignment(key, part):
    return shared_order(key)


def draw_counts(key, part):
    order_ids = shared_order(key)
    jitter = jax.random.randint(jax.random.fold_in(key, 11), (ORDERS,), 0, 4).astype(jnp.int32)
    jitter = jnp.where(order_ids == 0, 0, jitter)
    base_count = NK - (NK - NK_MIN) * order_ids // (ORDERS - 1)
    return jnp.maximum(NK_MIN, base_count - jitter).astype(jnp.int32)


def block_levels(stream_key, dims, split, low, top_value):
    gain, own = 1.0, jax.random.fold_in(stream_key, 6)
    for axis_at, blocks in split:
        heights = jnp.exp(jax.random.uniform(jax.random.fold_in(own, axis_at), (blocks,), jnp.float32, low / len(split), top_value / len(split)))
        gain = gain * jnp.repeat(heights, dims[axis_at] // blocks).reshape([-1 if axis == axis_at else 1 for axis in range(len(dims))])
    return gain


def noise(own_key, extent, scale, bound, shards=(), held_as=jnp.bfloat16):
    level = block_levels(own_key, extent, shards, -0.22, 0.18) if shards else 1.0
    values = jax.random.normal(own_key, extent, jnp.float32) * scale * level
    return jnp.minimum(jnp.maximum(values, -bound), bound).astype(held_as)


def setup_inputs(seed: int = 0) -> dict:
    arg_keys = jax.random.split(jax.random.key(seed), 7)
    return {
        "images": noise(arg_keys[0], (IMAGES, NR0, NA), 1.0, 6.0, ((0, 256),)),
        "radial_interp": noise(arg_keys[1], (NR0, NR), NR0 ** -0.5, 0.5),
        "assignment": draw_assignment(jax.random.fold_in(arg_keys[6], 71), 0),
        "counts": draw_counts(jax.random.fold_in(arg_keys[6], 71), 0),
        "radial_basis": noise(arg_keys[4], (ORDERS, NR, NK), NR ** -0.5, 0.5, ((0, 8),)),
        "eigenbasis": noise(arg_keys[5], (ORDERS, NK, NE), NK ** -0.5, 0.5, ((0, 8),)),
    }


def build_table(slot_orders, samples):
    angle_index = jnp.arange(samples, dtype=jnp.int32)[:, None]
    product = angle_index * slot_orders[None, :].astype(jnp.int32) % samples
    theta = product.astype(jnp.float32) * (2.0 * math.pi / samples)
    factor = 1.0 / math.sqrt(samples)
    return (jnp.concatenate([jnp.cos(theta), -jnp.sin(theta)], axis=1) * factor).astype(jnp.bfloat16)

def reference(images, radial_interp, assignment, counts, radial_basis, eigenbasis):
    dft_table = build_table(assignment, NA).astype(jnp.float32)
    kept_mask = (jnp.arange(NK, dtype=jnp.int32)[None, :] < counts[:, None]).astype(jnp.bfloat16)
    kept_basis = (radial_basis * kept_mask[:, None, :]).astype(jnp.float32)
    interp_wide = radial_interp.astype(jnp.float32)
    eigen_wide = eigenbasis.astype(jnp.float32)
    block_size = IMG_DEV * N_ORDER
    blocks = images.reshape(IMAGES // block_size, block_size, NR0, NA)

    def one_block(carry, block_images):
        polar_grid = jnp.einsum('isa,sr->ira', block_images.astype(jnp.float32), interp_wide).astype(jnp.bfloat16)
        spectrum = jnp.einsum('ira,ac->cir', polar_grid.astype(jnp.float32), dft_table).astype(jnp.bfloat16)
        spectrum = spectrum.reshape(2, ORDERS, block_size, NR).astype(jnp.float32)
        coefficients = jnp.einsum('pkir,krj->pkij', spectrum, kept_basis).astype(jnp.bfloat16).astype(jnp.float32)
        real_cov = jnp.einsum('pkij,pkil->kjl', coefficients, coefficients)
        imag_cov = jnp.einsum('kij,kil->kjl', coefficients[1], coefficients[0]) - jnp.einsum('kij,kil->kjl', coefficients[0], coefficients[1])
        projected_block = jnp.einsum('pkij,kje->pkie', coefficients, eigen_wide).astype(jnp.bfloat16)
        return (carry + jnp.stack([real_cov, imag_cov], 0), projected_block)
    start_cov = jnp.zeros((2, ORDERS, NK, NK), jnp.float32)
    summed_cov, projected_all = lax.scan(one_block, start_cov, blocks)
    projected = projected_all.transpose(1, 2, 0, 3, 4).reshape(2, ORDERS, IMAGES, NE)
    covariance = (summed_cov / IMAGES).transpose(1, 0, 2, 3).reshape(ORDERS, 2 * NK * NK)
    return (covariance, projected)
```

```python
import functools
import math

import numpy as np
import jax
import jax.numpy as jnp
from jax import lax
from jax.experimental import pallas as pl
from jax.experimental.pallas import tpu as pltpu
from jax.sharding import PartitionSpec as P

NY, NZ = 4, 8
NO = 8
GROUPS = 4
FIRST = 3
EXCHANGE = (4, 5, 2, 6, 3, 7, 1)


def angle_tables(samples, orders):
    product = np.arange(orders)[:, None] * np.arange(samples)[None, :] % samples
    theta = product * (2.0 * math.pi / samples)
    factor = 1.0 / math.sqrt(samples)
    both = np.stack([np.cos(theta), -np.sin(theta)]) * factor
    return both.astype(np.float32).astype(jnp.bfloat16)


def spectrum_kernel(x_ref, interp_ref, slots_ref, tables_ref, *rest):
    outs, table = rest[:-1], rest[-1]
    total = tables_ref.shape[1]
    split = total * FIRST // GROUPS

    @pl.when(pl.program_id(0) == 0)
    def _():
        me = lax.axis_index("order")
        y = lax.axis_index("dp") // NZ
        row = lax.broadcasted_iota(jnp.int32, (2 * total, total), 0)
        part, s = row & 1, row >> 1
        late = s >= split
        t = jnp.where(late, s - split, s)
        per = FIRST * 8
        d_first = (t * 2731) >> 16
        d = jnp.where(late, t >> 3, d_first)
        g = jnp.where(late, FIRST, (t - d_first * per) >> 3)
        dy, zl = (t >> 1) & 3, t & 1
        slot = (me ^ d) * (NY * NZ) + (y ^ dy) * NZ + g * 2 + zl
        lane = lax.broadcasted_iota(jnp.int32, (2 * total, total), 1)
        pick = (slot == lane).astype(jnp.bfloat16)
        order = lax.broadcasted_iota(jnp.int32, (total, total), 0)
        holds = (slots_ref[...] == order).astype(jnp.bfloat16)
        hot = lax.dot_general(
            pick, holds, (((1,), (1,)), ((), ())), preferred_element_type=jnp.float32
        ).astype(jnp.bfloat16)
        cosine = jnp.dot(hot, tables_ref[0], preferred_element_type=jnp.float32)
        sine = jnp.dot(hot, tables_ref[1], preferred_element_type=jnp.float32)
        odd = lax.broadcasted_iota(jnp.int32, cosine.shape, 0) & 1
        table[...] = jnp.where(odd == 1, sine, cosine).astype(jnp.bfloat16)

    n = x_ref.shape[0]
    interp = interp_ref[...]
    nodes = interp.shape[1]
    for i in range(0, n, 2):
        polar = jnp.concatenate(
            [
                lax.dot_general(
                    interp, x_ref[i + h], (((0,), (0,)), ((), ())),
                    preferred_element_type=jnp.float32,
                ).astype(jnp.bfloat16)
                for h in range(2)
            ],
            axis=0,
        )
        spec = lax.dot_general(
            table[...], polar, (((1,), (1,)), ((), ())), preferred_element_type=jnp.float32
        ).astype(jnp.bfloat16)
        base = 0
        for out in outs:
            rows = out.shape[1]
            for h in range(2):
                out[i + h] = spec[base : base + rows, h * nodes : (h + 1) * nodes]
            base += rows


def spectra(images, interp, assignment):
    count, radii, samples = images.shape
    nodes = interp.shape[1]
    total = assignment.shape[0]
    step = 4
    heights = [2 * total * FIRST // GROUPS // NO] * NO
    heights += [2 * total * (GROUPS - FIRST) // GROUPS // NO] * NO
    tables = jnp.asarray(angle_tables(samples, total))
    return pl.pallas_call(
        spectrum_kernel,
        grid=(count // step,),
        in_specs=[
            pl.BlockSpec((step, radii, samples), lambda i: (i, 0, 0)),
            pl.BlockSpec((radii, nodes), lambda i: (0, 0)),
            pl.BlockSpec((1, total), lambda i: (0, 0)),
            pl.BlockSpec((2, total, samples), lambda i: (0, 0, 0)),
        ],
        out_specs=[pl.BlockSpec((step, h, nodes), lambda i: (i, 0, 0)) for h in heights],
        out_shape=[jax.ShapeDtypeStruct((count, h, nodes), jnp.bfloat16) for h in heights],
        scratch_shapes=[pltpu.VMEM((2 * total, samples), jnp.bfloat16)],
        compiler_params=pltpu.CompilerParams(vmem_limit_bytes=48 << 20),
        cost_estimate=pl.CostEstimate(
            flops=2 * count * nodes * samples * (radii + 2 * total),
            bytes_accessed=4 * count * radii * samples,
            transcendentals=0,
        ),
        name="spectra",
    )(images, interp, assignment[None, :], tables)


def slot_kernel(scale, start, aliased, counts_ref, *refs):
    pieces, (basis_ref, eigen_ref) = refs[:NO], refs[NO : NO + 2]
    rest = refs[NO + 2 + aliased :]
    out_ref, covs, wide = rest[0], rest[1 : 1 + NY], rest[-1]
    me = lax.axis_index("order")
    y = lax.axis_index("dp") // NZ
    group = start + pl.program_id(0)
    images, rows, nodes = pieces[0].shape
    for d in range(NO):
        wide[d] = pieces[d][...].astype(jnp.float32).reshape(images * rows, nodes)
    width = basis_ref.shape[3]
    lane = lax.broadcasted_iota(jnp.int32, (nodes, width), 1)
    row = lax.broadcasted_iota(jnp.int32, (width, width), 0)
    col = lax.broadcasted_iota(jnp.int32, (width, width), 1)
    upper = row <= col
    for dy in range(NY):
        yy = y ^ dy
        for zl in range(2):
            limit = counts_ref[yy * NZ + group * 2 + zl]
            basis = jnp.where(lane < limit, basis_ref[yy, zl], 0)
            spec = jnp.concatenate(
                [
                    wide[me ^ j, pl.ds(dy * 4 + zl * 2 + p, images, stride=rows), :]
                    for p in range(2)
                    for j in range(NO)
                ],
                axis=0,
            ).astype(jnp.bfloat16)
            coef = jnp.dot(spec, basis, preferred_element_type=jnp.float32).astype(jnp.bfloat16)
            half = coef.shape[0] // 2
            pair = jnp.concatenate([coef[:half], coef[half:]], axis=1)
            gram = lax.dot_general(
                pair, pair, (((0,), (0,)), ((), ())), preferred_element_type=jnp.float32
            )
            real = gram[:width, :width] + gram[width:, width:]
            imag = gram[width:, :width] - gram[:width, width:]
            covs[dy][zl] = (jnp.where(upper, real, imag) * scale).astype(jnp.bfloat16)
            projected = jnp.dot(
                coef, eigen_ref[yy, zl], preferred_element_type=jnp.float32
            ).astype(jnp.bfloat16)
            out_ref[0, yy, zl] = projected[:half]
            out_ref[1, yy, zl] = projected[half:]


def slots(pieces, counts, basis, eigen, scale, start, groups, earlier=None):
    images, _, nodes = pieces[0].shape
    owned, _, width = basis.shape
    ends = eigen.shape[2]
    rows = 4 * NY
    total = NO * images
    aliased = 0 if earlier is None else 1
    block = pl.BlockSpec((images, rows, nodes), lambda g, c: (0, g, 0))
    weights = pl.BlockSpec((NY, 2, nodes, width), lambda g, c: (0, start + g, 0, 0))
    in_specs = [block] * NO + [weights, weights]
    args = list(pieces) + [basis.reshape(NY, NZ, nodes, width), eigen.reshape(NY, NZ, width, ends)]
    if aliased:
        in_specs.append(pl.BlockSpec(memory_space=pl.ANY))
        args.append(earlier)
    return pl.pallas_call(
        functools.partial(slot_kernel, scale, start, aliased),
        grid_spec=pltpu.PrefetchScalarGridSpec(
            num_scalar_prefetch=1,
            grid=(groups,),
            in_specs=in_specs,
            out_specs=[
                pl.BlockSpec((2, NY, 2, total, ends), lambda g, c: (0, 0, start + g, 0, 0))
            ]
            + [pl.BlockSpec((2, width, width), lambda g, c: (g, 0, 0))] * NY,
            scratch_shapes=[pltpu.VMEM((NO, images * rows, nodes), jnp.float32)],
        ),
        out_shape=[jax.ShapeDtypeStruct((2, NY, NZ, total, ends), jnp.bfloat16)]
        + [jax.ShapeDtypeStruct((2 * groups, width, width), jnp.bfloat16)] * NY,
        input_output_aliases={len(args): 0} if aliased else {},
        compiler_params=pltpu.CompilerParams(vmem_limit_bytes=48 << 20),
        cost_estimate=pl.CostEstimate(
            flops=groups * 8 * 8 * total * nodes * width,
            bytes_accessed=groups * 4 << 20,
            transcendentals=0,
        ),
        name="slots",
    )(counts, *args)


def finish_kernel(parts_ref, out_ref):
    packed = parts_ref[0].astype(jnp.float32)
    for i in range(1, parts_ref.shape[0]):
        packed += parts_ref[i].astype(jnp.float32)
    other = packed.T
    row = lax.broadcasted_iota(jnp.int32, packed.shape, 0)
    col = lax.broadcasted_iota(jnp.int32, packed.shape, 1)
    out_ref[0] = jnp.where(row <= col, packed, other)
    out_ref[1] = jnp.where(row > col, packed, jnp.where(row < col, -other, 0.0))


def body(images, radial_interp, assignment, counts, radial_basis, eigenbasis):
    owned = radial_basis.shape[0]
    width = radial_basis.shape[2]
    total = images.shape[0] * lax.axis_size("order") * lax.axis_size("dp")
    pieces = spectra(images, radial_interp, assignment)

    def exchange(own):
        got = {0: own[0]}
        for d in EXCHANGE:
            got[d] = lax.ppermute(own[d], "order", [(i, i ^ d) for i in range(NO)])
        return [got[d] for d in range(NO)]

    def gather_y(covs):
        moved = [covs[0]]
        for dy in (2, 1, 3):
            perm = [(i, i ^ (dy * NZ)) for i in range(NY * NZ)]
            moved.append(lax.ppermute(covs[dy], "dp", perm))
        return sum(m.astype(jnp.float32) for m in moved).astype(jnp.bfloat16)

    first = exchange(pieces[:NO])
    second = exchange(pieces[NO:])
    scale = 1.0 / total
    projected, *cov_first = slots(
        first, counts, radial_basis, eigenbasis, scale, 0, FIRST
    )
    sum_first = gather_y(cov_first)
    projected, *cov_second = slots(
        second, counts, radial_basis, eigenbasis, scale, FIRST, GROUPS - FIRST, projected
    )
    sum_second = gather_y(cov_second)
    parts = jnp.concatenate([sum_first, sum_second], axis=0)
    rings = [[y * NZ + z for z in range(NZ)] for y in range(NY)]
    parts = lax.all_to_all(parts, "dp", 0, 0, axis_index_groups=rings, tiled=True)
    covariance = pl.pallas_call(
        finish_kernel,
        out_shape=jax.ShapeDtypeStruct((2, width, width), jnp.float32),
        name="finish",
    )(parts)
    projected = projected.reshape(2, owned, projected.shape[3], projected.shape[4])
    return (covariance.reshape(1, 2 * width * width), projected)


def solution(mesh):
    placed = (
        P(("dp", "order"), None, None),
        P(),
        P(),
        P("order"),
        P("order", None, None),
        P("order", None, None),
    )
    return jax.shard_map(
        body,
        mesh=mesh,
        in_specs=placed,
        out_specs=(P(("order", "dp"), None), P(None, "order", "dp", None)),
        check_vma=False,
    )
```

```python
import functools
import math

import numpy as np
import jax
import jax.numpy as jnp
from jax import lax
from jax.experimental import pallas as pl
from jax.experimental.pallas import tpu as pltpu
from jax.sharding import PartitionSpec as P

NY, NZ = 4, 8
NO = 8
GROUPS = 4
FIRST = 3
SPLIT = (4, 5)
WHOLE = (2, 6, 3, 7, 1, 0)
HEIGHT = 16
STARTS = [GROUPS * HEIGHT * d for d in SPLIT + WHOLE]
STARTS += [GROUPS * HEIGHT * d + FIRST * HEIGHT for d in SPLIT]
HEIGHTS = [FIRST * HEIGHT] * len(SPLIT) + [GROUPS * HEIGHT] * len(WHOLE)
HEIGHTS += [(GROUPS - FIRST) * HEIGHT] * len(SPLIT)


def angle_tables(samples, orders):
    product = np.arange(orders)[:, None] * np.arange(samples)[None, :] % samples
    theta = product * (2.0 * math.pi / samples)
    factor = 1.0 / math.sqrt(samples)
    both = np.stack([np.cos(theta), -np.sin(theta)]) * factor
    return both.astype(np.float32).astype(jnp.bfloat16)


def spectrum_kernel(x_ref, interp_ref, slots_ref, tables_ref, *rest):
    outs, table = rest[:-1], rest[-1]
    total = tables_ref.shape[1]
    samples = tables_ref.shape[2]

    @pl.when(pl.program_id(0) == 0)
    def _():
        me = lax.axis_index("order")
        y = lax.axis_index("dp") // NZ
        s = lax.broadcasted_iota(jnp.int32, (total, total), 0)
        d, g, dy, zl = s >> 5, (s >> 3) & 3, (s >> 1) & 3, s & 1
        slot = (me ^ d) * (NY * NZ) + (y ^ dy) * NZ + g * 2 + zl
        lane = lax.broadcasted_iota(jnp.int32, (total, total), 1)
        pick = (slot == lane).astype(jnp.bfloat16)
        holds = (slots_ref[...] == s).astype(jnp.bfloat16)
        hot = lax.dot_general(
            pick, holds, (((1,), (1,)), ((), ())), preferred_element_type=jnp.float32
        ).astype(jnp.bfloat16)
        both = [
            jnp.dot(hot, tables_ref[p], preferred_element_type=jnp.float32).reshape(
                total // 8, 1, 8, samples
            )
            for p in range(2)
        ]
        table[...] = (
            jnp.concatenate(both, axis=1).reshape(2 * total, samples).astype(jnp.bfloat16)
        )

    n, radii = x_ref.shape[0], x_ref.shape[1]
    interp = interp_ref[...]
    nodes = interp.shape[1]
    zero = jnp.zeros_like(interp)
    both = jnp.concatenate(
        [jnp.concatenate([interp, zero], axis=1), jnp.concatenate([zero, interp], axis=1)], axis=0
    )
    first = pl.program_id(0) * n
    for i in range(0, n, 2):
        polar = lax.dot_general(
            x_ref[i : i + 2].reshape(2 * radii, samples), both, (((0,), (0,)), ((), ())),
            preferred_element_type=jnp.float32,
        ).astype(jnp.bfloat16)
        spec = jnp.dot(table[...], polar, preferred_element_type=jnp.float32).astype(jnp.bfloat16)
        for out, base in zip(outs, STARTS):
            rows = out.shape[1]
            for h in range(2):
                out[first + i + h] = spec[base : base + rows, h * nodes : (h + 1) * nodes]


def in_hbm(x):
    return pltpu.with_memory_space_constraint(x, pltpu.HBM)


def spectra(images, interp, assignment):
    count, radii, samples = images.shape
    nodes = interp.shape[1]
    total = assignment.shape[0]
    step = 8
    tables = jnp.asarray(angle_tables(samples, total))
    return pl.pallas_call(
        spectrum_kernel,
        grid=(count // step,),
        in_specs=[
            pl.BlockSpec((step, radii, samples), lambda i: (i, 0, 0)),
            pl.BlockSpec((radii, nodes), lambda i: (0, 0)),
            pl.BlockSpec((1, total), lambda i: (0, 0)),
            pl.BlockSpec((2, total, samples), lambda i: (0, 0, 0)),
        ],
        out_specs=[pl.BlockSpec(memory_space=pltpu.VMEM)] * len(HEIGHTS),
        out_shape=[jax.ShapeDtypeStruct((count, h, nodes), jnp.bfloat16) for h in HEIGHTS],
        scratch_shapes=[pltpu.VMEM((2 * total, samples), jnp.bfloat16)],
        compiler_params=pltpu.CompilerParams(vmem_limit_bytes=40 << 20),
        cost_estimate=pl.CostEstimate(
            flops=2 * count * nodes * samples * (radii + 2 * total),
            bytes_accessed=4 * count * radii * samples,
            transcendentals=0,
        ),
        name="spectra",
    )(*(in_hbm(x) for x in (images, interp, assignment[None, :], tables)))


def slot_kernel(scale, start, counts_ref, *refs):
    pieces, basis_ref = refs[:NO], refs[NO]
    coef_ref, covs, turned = refs[NO + 1], refs[NO + 2 : NO + 2 + NY], refs[-1]
    me = lax.axis_index("order")
    y = lax.axis_index("dp") // NZ
    group = start + pl.program_id(0)
    images, rows, nodes = pieces[0].shape
    for i, d in enumerate(SPLIT + WHOLE):
        turned[d] = jnp.swapaxes(pieces[i][...], 0, 1)
    width = basis_ref.shape[3]
    lane = lax.broadcasted_iota(jnp.int32, (nodes, width), 1)
    row = lax.broadcasted_iota(jnp.int32, (width, width), 0)
    col = lax.broadcasted_iota(jnp.int32, (width, width), 1)
    upper = row <= col
    for dy in range(NY):
        yy = y ^ dy
        for zl in range(2):
            limit = counts_ref[yy * NZ + group * 2 + zl]
            basis = jnp.where(lane < limit, basis_ref[yy, zl], 0)
            spec = jnp.concatenate(
                [
                    turned[me ^ j, p * 8 + dy * 2 + zl]
                    for p in range(2)
                    for j in range(NO)
                ],
                axis=0,
            )
            coef = jnp.dot(spec, basis, preferred_element_type=jnp.float32).astype(jnp.bfloat16)
            half = coef.shape[0] // 2
            coef_ref[0, yy, zl] = coef[:half]
            coef_ref[1, yy, zl] = coef[half:]
            pair = jnp.concatenate([coef[:half], coef[half:]], axis=1)
            gram = lax.dot_general(
                pair, pair, (((0,), (0,)), ((), ())), preferred_element_type=jnp.float32
            )
            real = gram[:width, :width] + gram[width:, width:]
            imag = gram[width:, :width] - gram[:width, width:]
            covs[dy][zl] = (jnp.where(upper, real, imag) * scale).astype(jnp.bfloat16)


def slots(pieces, counts, basis, scale, start, groups):
    images, _, nodes = pieces[0].shape
    _, _, _, width = basis.shape
    rows = HEIGHT
    total = NO * images
    part = pl.BlockSpec((images, rows, nodes), lambda g, c: (0, g, 0))
    whole = pl.BlockSpec((images, rows, nodes), lambda g, c: (0, start + g, 0))
    weights = pl.BlockSpec((NY, 2, nodes, width), lambda g, c: (0, start + g, 0, 0))
    return pl.pallas_call(
        functools.partial(slot_kernel, scale, start),
        grid_spec=pltpu.PrefetchScalarGridSpec(
            num_scalar_prefetch=1,
            grid=(groups,),
            in_specs=[part] * len(SPLIT) + [whole] * len(WHOLE) + [weights],
            out_specs=[pl.BlockSpec((2, NY, 2, total, width), lambda g, c: (0, 0, g, 0, 0))]
            + [pl.BlockSpec((2, width, width), lambda g, c: (g, 0, 0))] * NY,
            scratch_shapes=[pltpu.VMEM((NO, rows, images, nodes), jnp.bfloat16)],
        ),
        out_shape=[pltpu.HBM((2, NY, 2 * groups, total, width), jnp.bfloat16)]
        + [jax.ShapeDtypeStruct((2 * groups, width, width), jnp.bfloat16)] * NY,
        compiler_params=pltpu.CompilerParams(vmem_limit_bytes=32 << 20),
        cost_estimate=pl.CostEstimate(
            flops=groups * 64 * 6 * total * nodes * width,
            bytes_accessed=groups * 3 << 20,
            transcendentals=0,
        ),
        name="slots",
    )(counts, *pieces, basis)


def project_kernel(first_ref, second_ref, eigen_ref, out_ref):
    groups = first_ref.shape[2] // 2

    def run(coef_ref):
        for y in range(NY):
            for zl in range(2):
                for p in range(2):
                    out_ref[p, y, zl] = jnp.dot(
                        coef_ref[p, y, zl], eigen_ref[y, zl], preferred_element_type=jnp.float32
                    ).astype(jnp.bfloat16)

    late = pl.program_id(0) >= FIRST

    @pl.when(jnp.logical_not(late))
    def _():
        run(first_ref)

    @pl.when(late)
    def _():
        run(second_ref)


def project(first, second, eigen):
    _, _, _, total, width = first.shape
    ends = eigen.shape[3]
    held = (2, NY, 2, total, width)
    return pl.pallas_call(
        project_kernel,
        grid=(GROUPS,),
        in_specs=[
            pl.BlockSpec(held, lambda g: (0, 0, jnp.minimum(g, FIRST - 1), 0, 0)),
            pl.BlockSpec(held, lambda g: (0, 0, jnp.maximum(g - FIRST, 0), 0, 0)),
            pl.BlockSpec((NY, 2, width, ends), lambda g: (0, g, 0, 0)),
        ],
        out_specs=pl.BlockSpec((2, NY, 2, total, ends), lambda g: (0, 0, g, 0, 0)),
        out_shape=jax.ShapeDtypeStruct((2, NY, NZ, total, ends), jnp.bfloat16),
        compiler_params=pltpu.CompilerParams(vmem_limit_bytes=32 << 20),
        cost_estimate=pl.CostEstimate(
            flops=4 * NY * NZ * total * width * ends, bytes_accessed=9 << 20, transcendentals=0
        ),
        name="project",
    )(in_hbm(first), in_hbm(second), in_hbm(eigen))


def join_kernel(*refs):
    ins, out_ref = refs[:-1], refs[-1]
    done = 0
    for part in (ins[:NY], ins[NY:]):
        held = part[0].shape[0]
        added = part[0][...].astype(jnp.float32)
        for moved in part[1:]:
            added += moved[...].astype(jnp.float32)
        out_ref[done : done + held] = added.astype(jnp.bfloat16)
        done += held


def finish_kernel(parts_ref, out_ref):
    packed = parts_ref[0].astype(jnp.float32)
    for i in range(1, parts_ref.shape[0]):
        packed += parts_ref[i].astype(jnp.float32)
    other = packed.T
    row = lax.broadcasted_iota(jnp.int32, packed.shape, 0)
    col = lax.broadcasted_iota(jnp.int32, packed.shape, 1)
    out_ref[0] = jnp.where(row <= col, packed, other)
    out_ref[1] = jnp.where(row > col, packed, jnp.where(row < col, -other, 0.0))


def body(images, radial_interp, assignment, counts, radial_basis, eigenbasis):
    owned = radial_basis.shape[0]
    width = radial_basis.shape[2]
    total = images.shape[0] * lax.axis_size("order") * lax.axis_size("dp")
    pieces = spectra(images, radial_interp, assignment)

    basis = radial_basis.reshape(NY, NZ, radial_basis.shape[1], width)
    eigen = eigenbasis.reshape(NY, NZ, width, eigenbasis.shape[2])

    def exchange(own, partners):
        return [
            lax.ppermute(piece, "order", [(i, i ^ d) for i in range(NO)])
            for piece, d in zip(own, partners)
        ]

    def to_y(covs):
        return [
            lax.ppermute(covs[dy], "dp", [(i, i ^ (dy * NZ)) for i in range(NY * NZ)])
            for dy in range(1, NY)
        ]

    scale = 1.0 / total
    far, near = len(SPLIT), len(SPLIT) + len(WHOLE)
    first = exchange(pieces[:far], SPLIT)
    whole = exchange(pieces[far : near - 1], WHOLE) + [pieces[near - 1]]
    *gated, first[0], first[1] = lax.optimization_barrier(tuple(pieces[near:]) + tuple(first))
    second = exchange(gated, SPLIT) + whole
    first += whole
    coef_first, *cov_first = slots(first, counts, basis, scale, 0, FIRST)
    moved_first = to_y(cov_first)
    coef_second, *cov_second = slots(second, counts, basis, scale, FIRST, GROUPS - FIRST)
    moved_second = to_y(cov_second)
    projected = project(coef_first, coef_second, eigen)
    parts = pl.pallas_call(
        join_kernel,
        out_shape=jax.ShapeDtypeStruct((NZ, width, width), jnp.bfloat16),
        compiler_params=pltpu.CompilerParams(vmem_limit_bytes=8 << 20),
        name="join",
    )(cov_first[0], *moved_first, cov_second[0], *moved_second)
    rings = [[y * NZ + z for z in range(NZ)] for y in range(NY)]
    parts = lax.all_to_all(parts, "dp", 0, 0, axis_index_groups=rings, tiled=True)
    covariance = pl.pallas_call(
        finish_kernel,
        out_shape=jax.ShapeDtypeStruct((2, width, width), jnp.float32),
        compiler_params=pltpu.CompilerParams(vmem_limit_bytes=8 << 20),
        name="finish",
    )(parts)
    projected = projected.reshape(2, owned, projected.shape[3], projected.shape[4])
    return (covariance.reshape(1, 2 * width * width), projected)


def solution(mesh):
    placed = (
        P(("dp", "order"), None, None),
        P(),
        P(),
        P("order"),
        P("order", None, None),
        P("order", None, None),
    )
    return jax.shard_map(
        body,
        mesh=mesh,
        in_specs=placed,
        out_specs=(P(("order", "dp"), None), P(None, "order", "dp", None)),
        check_vma=False,
    )
```

```python
import functools
import math

import numpy as np
import jax
import jax.numpy as jnp
from jax import lax
from jax.experimental import pallas as pl
from jax.experimental.pallas import tpu as pltpu
from jax.sharding import PartitionSpec as P

NY, NZ = 4, 8
NO = 8
GROUPS = 4
FIRST = 3
SPLIT = (4, 5)
WHOLE = (2, 6, 3, 7, 1, 0)
HEIGHT = 16
STARTS = [GROUPS * HEIGHT * d for d in SPLIT + WHOLE]
STARTS += [GROUPS * HEIGHT * d + FIRST * HEIGHT for d in SPLIT]
HEIGHTS = [FIRST * HEIGHT] * len(SPLIT) + [GROUPS * HEIGHT] * len(WHOLE)
HEIGHTS += [(GROUPS - FIRST) * HEIGHT] * len(SPLIT)


def angle_tables(samples, orders):
    product = np.arange(orders)[:, None] * np.arange(samples)[None, :] % samples
    theta = product * (2.0 * math.pi / samples)
    factor = 1.0 / math.sqrt(samples)
    both = np.stack([np.cos(theta), -np.sin(theta)]) * factor
    return both.astype(np.float32).astype(jnp.bfloat16)


def spectrum_kernel(x_ref, interp_ref, slots_ref, tables_ref, *rest):
    outs, table = rest[:-1], rest[-1]
    total = tables_ref.shape[1]
    samples = tables_ref.shape[2]

    @pl.when(pl.program_id(0) == 0)
    def _():
        me = lax.axis_index("order")
        y = lax.axis_index("dp") // NZ
        s = lax.broadcasted_iota(jnp.int32, (total, total), 0)
        d, g, dy, zl = s >> 5, (s >> 3) & 3, (s >> 1) & 3, s & 1
        slot = (me ^ d) * (NY * NZ) + (y ^ dy) * NZ + g * 2 + zl
        lane = lax.broadcasted_iota(jnp.int32, (total, total), 1)
        pick = (slot == lane).astype(jnp.bfloat16)
        holds = (slots_ref[...] == s).astype(jnp.bfloat16)
        hot = lax.dot_general(
            pick, holds, (((1,), (1,)), ((), ())), preferred_element_type=jnp.float32
        ).astype(jnp.bfloat16)
        both = [
            jnp.dot(hot, tables_ref[p], preferred_element_type=jnp.float32).reshape(
                total // 8, 1, 8, samples
            )
            for p in range(2)
        ]
        table[...] = (
            jnp.concatenate(both, axis=1).reshape(2 * total, samples).astype(jnp.bfloat16)
        )

    n, radii = x_ref.shape[0], x_ref.shape[1]
    interp = interp_ref[...]
    nodes = interp.shape[1]
    zero = jnp.zeros_like(interp)
    both = jnp.concatenate(
        [jnp.concatenate([interp, zero], axis=1), jnp.concatenate([zero, interp], axis=1)], axis=0
    )
    first = pl.program_id(0) * n
    for i in range(0, n, 2):
        polar = lax.dot_general(
            x_ref[i : i + 2].reshape(2 * radii, samples), both, (((0,), (0,)), ((), ())),
            preferred_element_type=jnp.float32,
        ).astype(jnp.bfloat16)
        spec = jnp.dot(table[...], polar, preferred_element_type=jnp.float32).astype(jnp.bfloat16)
        for out, base in zip(outs, STARTS):
            rows = out.shape[1]
            for h in range(2):
                out[first + i + h] = spec[base : base + rows, h * nodes : (h + 1) * nodes]


def in_hbm(x):
    return pltpu.with_memory_space_constraint(x, pltpu.HBM)


def spectra(images, interp, assignment):
    count, radii, samples = images.shape
    nodes = interp.shape[1]
    total = assignment.shape[0]
    step = 16
    tables = jnp.asarray(angle_tables(samples, total))
    return pl.pallas_call(
        spectrum_kernel,
        grid=(count // step,),
        in_specs=[
            pl.BlockSpec((step, radii, samples), lambda i: (i, 0, 0)),
            pl.BlockSpec((radii, nodes), lambda i: (0, 0)),
            pl.BlockSpec((1, total), lambda i: (0, 0)),
            pl.BlockSpec((2, total, samples), lambda i: (0, 0, 0)),
        ],
        out_specs=[pl.BlockSpec(memory_space=pltpu.VMEM)] * len(HEIGHTS),
        out_shape=[jax.ShapeDtypeStruct((count, h, nodes), jnp.bfloat16) for h in HEIGHTS],
        scratch_shapes=[pltpu.VMEM((2 * total, samples), jnp.bfloat16)],
        compiler_params=pltpu.CompilerParams(vmem_limit_bytes=40 << 20),
        cost_estimate=pl.CostEstimate(
            flops=2 * count * nodes * samples * (radii + 2 * total),
            bytes_accessed=4 * count * radii * samples,
            transcendentals=0,
        ),
        name="spectra",
    )(*(in_hbm(x) for x in (images, interp, assignment[None, :], tables)))


def slot_kernel(scale, start, aliased, counts_ref, *refs):
    pieces, basis_ref = refs[:NO], refs[NO]
    refs = refs[NO + 1 + aliased :]
    coef_ref, covs, turned = refs[0], refs[1 : 1 + NY], refs[-1]
    me = lax.axis_index("order")
    y = lax.axis_index("dp") // NZ
    group = start + pl.program_id(0)
    images, rows, nodes = pieces[0].shape[0], HEIGHT, pieces[0].shape[2]
    for i, d in enumerate(SPLIT + WHOLE):
        at = pl.multiple_of((group if d in WHOLE else group - start) * rows, rows)
        turned[d] = jnp.swapaxes(pieces[i][:, pl.ds(at, rows), :], 0, 1)
    width = basis_ref.shape[3]
    lane = lax.broadcasted_iota(jnp.int32, (nodes, width), 1)
    row = lax.broadcasted_iota(jnp.int32, (width, width), 0)
    col = lax.broadcasted_iota(jnp.int32, (width, width), 1)
    upper = row <= col
    for dy in range(NY):
        yy = y ^ dy
        for zl in range(2):
            limit = counts_ref[yy * NZ + group * 2 + zl]
            basis = jnp.where(lane < limit, basis_ref[yy, group * 2 + zl], 0)
            spec = jnp.concatenate(
                [
                    turned[me ^ j, p * 8 + dy * 2 + zl]
                    for p in range(2)
                    for j in range(NO)
                ],
                axis=0,
            )
            coef = jnp.dot(spec, basis, preferred_element_type=jnp.float32).astype(jnp.bfloat16)
            half = coef.shape[0] // 2
            coef_ref[0, yy, zl] = coef[:half]
            coef_ref[1, yy, zl] = coef[half:]
            pair = jnp.concatenate([coef[:half], coef[half:]], axis=1)
            gram = lax.dot_general(
                pair, pair, (((0,), (0,)), ((), ())), preferred_element_type=jnp.float32
            )
            real = gram[:width, :width] + gram[width:, width:]
            imag = gram[width:, :width] - gram[:width, width:]
            covs[dy][zl] = (jnp.where(upper, real, imag) * scale).astype(jnp.bfloat16)


def slots(pieces, counts, basis, scale, start, groups, covs=()):
    images, _, nodes = pieces[0].shape
    _, _, _, width = basis.shape
    rows = HEIGHT
    total = NO * images
    return pl.pallas_call(
        functools.partial(slot_kernel, scale, start, len(covs)),
        grid_spec=pltpu.PrefetchScalarGridSpec(
            num_scalar_prefetch=1,
            grid=(groups,),
            in_specs=[pl.BlockSpec(memory_space=pltpu.VMEM)] * (NO + 1)
            + [pl.BlockSpec(memory_space=pl.ANY)] * len(covs),
            out_specs=[pl.BlockSpec((2, NY, 2, total, width), lambda g, c: (0, 0, g, 0, 0))]
            + [pl.BlockSpec((2, width, width), lambda g, c: (start + g, 0, 0))] * NY,
            scratch_shapes=[pltpu.VMEM((NO, rows, images, nodes), jnp.bfloat16)],
        ),
        out_shape=[pltpu.HBM((2, NY, 2 * groups, total, width), jnp.bfloat16)]
        + [jax.ShapeDtypeStruct((NZ, width, width), jnp.bfloat16)] * NY,
        input_output_aliases={NO + 2 + i: 1 + i for i in range(len(covs))},
        compiler_params=pltpu.CompilerParams(vmem_limit_bytes=32 << 20),
        cost_estimate=pl.CostEstimate(
            flops=groups * 64 * 6 * total * nodes * width,
            bytes_accessed=groups * 3 << 20,
            transcendentals=0,
        ),
        name="slots",
    )(counts, *pieces, basis, *covs)


def project_kernel(first_ref, second_ref, eigen_ref, out_ref):
    groups = first_ref.shape[2] // 2

    def run(coef_ref):
        for y in range(NY):
            for zl in range(2):
                for p in range(2):
                    out_ref[p, y, zl] = jnp.dot(
                        coef_ref[p, y, zl], eigen_ref[y, zl], preferred_element_type=jnp.float32
                    ).astype(jnp.bfloat16)

    late = pl.program_id(0) >= FIRST

    @pl.when(jnp.logical_not(late))
    def _():
        run(first_ref)

    @pl.when(late)
    def _():
        run(second_ref)


def project(first, second, eigen):
    _, _, _, total, width = first.shape
    ends = eigen.shape[3]
    held = (2, NY, 2, total, width)
    return pl.pallas_call(
        project_kernel,
        grid=(GROUPS,),
        in_specs=[
            pl.BlockSpec(held, lambda g: (0, 0, jnp.minimum(g, FIRST - 1), 0, 0)),
            pl.BlockSpec(held, lambda g: (0, 0, jnp.maximum(g - FIRST, 0), 0, 0)),
            pl.BlockSpec((NY, 2, width, ends), lambda g: (0, g, 0, 0)),
        ],
        out_specs=pl.BlockSpec((2, NY, 2, total, ends), lambda g: (0, 0, g, 0, 0)),
        out_shape=jax.ShapeDtypeStruct((2, NY, NZ, total, ends), jnp.bfloat16),
        compiler_params=pltpu.CompilerParams(vmem_limit_bytes=32 << 20),
        cost_estimate=pl.CostEstimate(
            flops=4 * NY * NZ * total * width * ends, bytes_accessed=9 << 20, transcendentals=0
        ),
        name="project",
    )(in_hbm(first), in_hbm(second), in_hbm(eigen))


def join_kernel(*refs):
    added = refs[0][...].astype(jnp.float32)
    for moved in refs[1:-1]:
        added += moved[...].astype(jnp.float32)
    refs[-1][...] = added.astype(jnp.bfloat16)


def finish_kernel(parts_ref, out_ref):
    packed = parts_ref[0].astype(jnp.float32)
    for i in range(1, parts_ref.shape[0]):
        packed += parts_ref[i].astype(jnp.float32)
    other = packed.T
    row = lax.broadcasted_iota(jnp.int32, packed.shape, 0)
    col = lax.broadcasted_iota(jnp.int32, packed.shape, 1)
    out_ref[0] = jnp.where(row <= col, packed, other)
    out_ref[1] = jnp.where(row > col, packed, jnp.where(row < col, -other, 0.0))


def body(images, radial_interp, assignment, counts, radial_basis, eigenbasis):
    owned = radial_basis.shape[0]
    width = radial_basis.shape[2]
    total = images.shape[0] * lax.axis_size("order") * lax.axis_size("dp")
    pieces = spectra(images, radial_interp, assignment)

    basis = radial_basis.reshape(NY, NZ, radial_basis.shape[1], width)
    eigen = eigenbasis.reshape(NY, NZ, width, eigenbasis.shape[2])

    def exchange(own, partners):
        return [
            lax.ppermute(piece, "order", [(i, i ^ d) for i in range(NO)])
            for piece, d in zip(own, partners)
        ]

    def to_y(covs):
        return [
            lax.ppermute(covs[dy], "dp", [(i, i ^ (dy * NZ)) for i in range(NY * NZ)])
            for dy in (2, 1, 3)
        ]

    scale = 1.0 / total
    far, near = len(SPLIT), len(SPLIT) + len(WHOLE)
    first = exchange(pieces[:far], SPLIT)
    whole = exchange(pieces[far : near - 1], WHOLE) + [pieces[near - 1]]
    *gated, first[0], first[1] = lax.optimization_barrier(tuple(pieces[near:]) + tuple(first))
    second = exchange(gated, SPLIT) + whole
    first += whole
    coef_first, *covs = slots(first, counts, basis, scale, 0, FIRST)
    coef_second, *covs = slots(second, counts, basis, scale, FIRST, GROUPS - FIRST, covs)
    projected = project(coef_first, coef_second, eigen)
    parts = pl.pallas_call(
        join_kernel,
        out_shape=jax.ShapeDtypeStruct((NZ, width, width), jnp.bfloat16),
        compiler_params=pltpu.CompilerParams(vmem_limit_bytes=8 << 20),
        name="join",
    )(covs[0], *to_y(covs))
    rings = [[y * NZ + z for z in range(NZ)] for y in range(NY)]
    parts = lax.all_to_all(parts, "dp", 0, 0, axis_index_groups=rings, tiled=True)
    covariance = pl.pallas_call(
        finish_kernel,
        out_shape=jax.ShapeDtypeStruct((2, width, width), jnp.float32),
        compiler_params=pltpu.CompilerParams(vmem_limit_bytes=8 << 20),
        name="finish",
    )(parts)
    projected = projected.reshape(2, owned, projected.shape[3], projected.shape[4])
    return (covariance.reshape(1, 2 * width * width), projected)


def solution(mesh):
    placed = (
        P(("dp", "order"), None, None),
        P(),
        P(),
        P("order"),
        P("order", None, None),
        P("order", None, None),
    )
    return jax.shard_map(
        body,
        mesh=mesh,
        in_specs=placed,
        out_specs=(P(("order", "dp"), None), P(None, "order", "dp", None)),
        check_vma=False,
    )
```

```python
import functools
import math

import numpy as np
import jax
import jax.numpy as jnp
from jax import lax
from jax.experimental import pallas as pl
from jax.experimental.pallas import tpu as pltpu
from jax.sharding import PartitionSpec as P

NY, NZ = 4, 8
NO = 8
GROUPS = 4
FIRST = 3
SPLIT = (4, 5)
WHOLE = (2, 6, 3, 7, 1, 0)
HEIGHT = 16
STARTS = [GROUPS * HEIGHT * d for d in SPLIT + WHOLE]
STARTS += [GROUPS * HEIGHT * d + FIRST * HEIGHT for d in SPLIT]
HEIGHTS = [FIRST * HEIGHT] * len(SPLIT) + [GROUPS * HEIGHT] * len(WHOLE)
HEIGHTS += [(GROUPS - FIRST) * HEIGHT] * len(SPLIT)


def angle_tables(samples, orders):
    product = np.arange(orders)[:, None] * np.arange(samples)[None, :] % samples
    theta = product * (2.0 * math.pi / samples)
    factor = 1.0 / math.sqrt(samples)
    both = np.stack([np.cos(theta), -np.sin(theta)]) * factor
    return both.astype(np.float32).astype(jnp.bfloat16)


def spectrum_kernel(x_ref, interp_ref, slots_ref, tables_ref, *rest):
    outs, table = rest[:-1], rest[-1]
    total = tables_ref.shape[1]
    samples = tables_ref.shape[2]

    @pl.when(pl.program_id(0) == 0)
    def _():
        me = lax.axis_index("order")
        y = lax.axis_index("dp") // NZ
        s = lax.broadcasted_iota(jnp.int32, (total, total), 0)
        d, g, dy, zl = s >> 5, (s >> 3) & 3, (s >> 1) & 3, s & 1
        slot = (me ^ d) * (NY * NZ) + (y ^ dy) * NZ + g * 2 + zl
        lane = lax.broadcasted_iota(jnp.int32, (total, total), 1)
        pick = (slot == lane).astype(jnp.bfloat16)
        holds = (slots_ref[...] == s).astype(jnp.bfloat16)
        hot = lax.dot_general(
            pick, holds, (((1,), (1,)), ((), ())), preferred_element_type=jnp.float32
        ).astype(jnp.bfloat16)
        both = [
            jnp.dot(hot, tables_ref[p], preferred_element_type=jnp.float32).reshape(
                total // 8, 1, 8, samples
            )
            for p in range(2)
        ]
        table[...] = (
            jnp.concatenate(both, axis=1).reshape(2 * total, samples).astype(jnp.bfloat16)
        )

    n, radii = x_ref.shape[0], x_ref.shape[1]
    interp = interp_ref[...]
    nodes = interp.shape[1]
    zero = jnp.zeros_like(interp)
    both = jnp.concatenate(
        [jnp.concatenate([interp, zero], axis=1), jnp.concatenate([zero, interp], axis=1)], axis=0
    )
    first = pl.program_id(0) * n
    for i in range(0, n, 2):
        polar = lax.dot_general(
            x_ref[i : i + 2].reshape(2 * radii, samples), both, (((0,), (0,)), ((), ())),
            preferred_element_type=jnp.float32,
        ).astype(jnp.bfloat16)
        spec = jnp.dot(table[...], polar, preferred_element_type=jnp.float32).astype(jnp.bfloat16)
        for out, base in zip(outs, STARTS):
            rows = out.shape[1]
            for h in range(2):
                out[first + i + h] = spec[base : base + rows, h * nodes : (h + 1) * nodes]


def in_hbm(x):
    return pltpu.with_memory_space_constraint(x, pltpu.HBM)


def spectra(images, interp, assignment):
    count, radii, samples = images.shape
    nodes = interp.shape[1]
    total = assignment.shape[0]
    step = 16
    tables = jnp.asarray(angle_tables(samples, total))
    return pl.pallas_call(
        spectrum_kernel,
        grid=(count // step,),
        in_specs=[
            pl.BlockSpec((step, radii, samples), lambda i: (i, 0, 0)),
            pl.BlockSpec((radii, nodes), lambda i: (0, 0)),
            pl.BlockSpec((1, total), lambda i: (0, 0)),
            pl.BlockSpec((2, total, samples), lambda i: (0, 0, 0)),
        ],
        out_specs=[pl.BlockSpec(memory_space=pltpu.VMEM)] * len(HEIGHTS),
        out_shape=[jax.ShapeDtypeStruct((count, h, nodes), jnp.bfloat16) for h in HEIGHTS],
        scratch_shapes=[pltpu.VMEM((2 * total, samples), jnp.bfloat16)],
        compiler_params=pltpu.CompilerParams(vmem_limit_bytes=40 << 20),
        cost_estimate=pl.CostEstimate(
            flops=2 * count * nodes * samples * (radii + 2 * total),
            bytes_accessed=4 * count * radii * samples,
            transcendentals=0,
        ),
        name="spectra",
    )(*(in_hbm(x) for x in (images, interp, assignment[None, :], tables)))


def slot_kernel(scale, start, aliased, counts_ref, *refs):
    pieces, basis_ref = refs[:NO], refs[NO]
    refs = refs[NO + 1 + aliased :]
    coef_ref, covs, turned = refs[0], refs[1 : 1 + NY], refs[-1]
    me = lax.axis_index("order")
    y = lax.axis_index("dp") // NZ
    group = start + pl.program_id(0)
    images, rows, nodes = pieces[0].shape[0], HEIGHT, pieces[0].shape[2]
    for i, d in enumerate(SPLIT + WHOLE):
        at = pl.multiple_of((group if d in WHOLE else group - start) * rows, rows)
        turned[d] = jnp.swapaxes(pieces[i][:, pl.ds(at, rows), :], 0, 1)
    width = basis_ref.shape[3]
    lane = lax.broadcasted_iota(jnp.int32, (nodes, width), 1)
    row = lax.broadcasted_iota(jnp.int32, (width, width), 0)
    col = lax.broadcasted_iota(jnp.int32, (width, width), 1)
    upper = row <= col
    for dy in range(NY):
        yy = y ^ dy
        for zl in range(2):
            limit = counts_ref[yy * NZ + group * 2 + zl]
            basis = jnp.where(lane < limit, basis_ref[yy, group * 2 + zl], 0)
            spec = jnp.concatenate(
                [
                    turned[me ^ j, p * 8 + dy * 2 + zl]
                    for p in range(2)
                    for j in range(NO)
                ],
                axis=0,
            )
            coef = jnp.dot(spec, basis, preferred_element_type=jnp.float32).astype(jnp.bfloat16)
            half = coef.shape[0] // 2
            coef_ref[0, yy, zl] = coef[:half]
            coef_ref[1, yy, zl] = coef[half:]
            pair = jnp.concatenate([coef[:half], coef[half:]], axis=1)
            gram = lax.dot_general(
                pair, pair, (((0,), (0,)), ((), ())), preferred_element_type=jnp.float32
            )
            real = gram[:width, :width] + gram[width:, width:]
            imag = gram[width:, :width] - gram[:width, width:]
            covs[dy][zl] = (jnp.where(upper, real, imag) * scale).astype(jnp.bfloat16)


def slots(pieces, counts, basis, scale, start, groups, covs=()):
    images, _, nodes = pieces[0].shape
    _, _, _, width = basis.shape
    rows = HEIGHT
    total = NO * images
    return pl.pallas_call(
        functools.partial(slot_kernel, scale, start, len(covs)),
        grid_spec=pltpu.PrefetchScalarGridSpec(
            num_scalar_prefetch=1,
            grid=(groups,),
            in_specs=[pl.BlockSpec(memory_space=pltpu.VMEM)] * (NO + 1)
            + [pl.BlockSpec(memory_space=pl.ANY)] * len(covs),
            out_specs=[pl.BlockSpec((2, NY, 2, total, width), lambda g, c: (0, 0, g, 0, 0))]
            + [pl.BlockSpec((2, width, width), lambda g, c: (start + g, 0, 0))] * NY,
            scratch_shapes=[pltpu.VMEM((NO, rows, images, nodes), jnp.bfloat16)],
        ),
        out_shape=[pltpu.HBM((2, NY, 2 * groups, total, width), jnp.bfloat16)]
        + [jax.ShapeDtypeStruct((NZ, width, width), jnp.bfloat16)] * NY,
        input_output_aliases={NO + 2 + i: 1 + i for i in range(len(covs))},
        compiler_params=pltpu.CompilerParams(vmem_limit_bytes=32 << 20),
        cost_estimate=pl.CostEstimate(
            flops=groups * 64 * 6 * total * nodes * width,
            bytes_accessed=groups * 3 << 20,
            transcendentals=0,
        ),
        name="slots",
    )(counts, *pieces, basis, *covs)


def project_kernel(first_ref, second_ref, eigen_ref, out_ref):
    groups = first_ref.shape[2] // 2

    def run(coef_ref):
        for y in range(NY):
            for zl in range(2):
                for p in range(2):
                    out_ref[p, y, zl] = jnp.dot(
                        coef_ref[p, y, zl], eigen_ref[y, zl], preferred_element_type=jnp.float32
                    ).astype(jnp.bfloat16)

    late = pl.program_id(0) >= FIRST

    @pl.when(jnp.logical_not(late))
    def _():
        run(first_ref)

    @pl.when(late)
    def _():
        run(second_ref)


def project(first, second, eigen):
    _, _, _, total, width = first.shape
    ends = eigen.shape[3]
    held = (2, NY, 2, total, width)
    return pl.pallas_call(
        project_kernel,
        grid=(GROUPS,),
        in_specs=[
            pl.BlockSpec(held, lambda g: (0, 0, jnp.minimum(g, FIRST - 1), 0, 0)),
            pl.BlockSpec(held, lambda g: (0, 0, jnp.maximum(g - FIRST, 0), 0, 0)),
            pl.BlockSpec((NY, 2, width, ends), lambda g: (0, g, 0, 0)),
        ],
        out_specs=pl.BlockSpec((2, NY, 2, total, ends), lambda g: (0, 0, g, 0, 0)),
        out_shape=jax.ShapeDtypeStruct((2, NY, NZ, total, ends), jnp.bfloat16),
        compiler_params=pltpu.CompilerParams(vmem_limit_bytes=32 << 20),
        cost_estimate=pl.CostEstimate(
            flops=4 * NY * NZ * total * width * ends, bytes_accessed=9 << 20, transcendentals=0
        ),
        name="project",
    )(in_hbm(first), in_hbm(second), in_hbm(eigen))


def join_kernel(*refs):
    added = refs[0][...].astype(jnp.float32)
    for moved in refs[1:-1]:
        added += moved[...].astype(jnp.float32)
    refs[-1][...] = added.astype(jnp.bfloat16)


def finish_kernel(parts_ref, out_ref):
    packed = parts_ref[0].astype(jnp.float32)
    for i in range(1, parts_ref.shape[0]):
        packed += parts_ref[i].astype(jnp.float32)
    other = packed.T
    row = lax.broadcasted_iota(jnp.int32, packed.shape, 0)
    col = lax.broadcasted_iota(jnp.int32, packed.shape, 1)
    out_ref[0] = jnp.where(row <= col, packed, other)
    out_ref[1] = jnp.where(row > col, packed, jnp.where(row < col, -other, 0.0))


def body(images, radial_interp, assignment, counts, radial_basis, eigenbasis):
    owned = radial_basis.shape[0]
    width = radial_basis.shape[2]
    total = images.shape[0] * lax.axis_size("order") * lax.axis_size("dp")
    pieces = spectra(images, radial_interp, assignment)

    basis = radial_basis.reshape(NY, NZ, radial_basis.shape[1], width)
    eigen = eigenbasis.reshape(NY, NZ, width, eigenbasis.shape[2])

    def exchange(own, partners):
        return [
            lax.ppermute(piece, "order", [(i, i ^ d) for i in range(NO)])
            for piece, d in zip(own, partners)
        ]

    def to_y(covs):
        return [
            lax.ppermute(covs[dy], "dp", [(i, i ^ (dy * NZ)) for i in range(NY * NZ)])
            for dy in (2, 1, 3)
        ]

    scale = 1.0 / total
    far, near = len(SPLIT), len(SPLIT) + len(WHOLE)
    first = exchange(pieces[:far], SPLIT)
    whole = exchange(pieces[far : near - 1], WHOLE) + [pieces[near - 1]]
    *gated, first[0], first[1] = lax.optimization_barrier(tuple(pieces[near:]) + tuple(first))
    second = exchange(gated, SPLIT) + whole
    first += whole
    coef_first, *covs = slots(first, counts, basis, scale, 0, FIRST)
    coef_second, *covs = slots(second, counts, basis, scale, FIRST, GROUPS - FIRST, covs)
    projected = project(coef_first, coef_second, eigen)
    parts = pl.pallas_call(
        join_kernel,
        out_shape=jax.ShapeDtypeStruct((NZ, width, width), jnp.bfloat16),
        compiler_params=pltpu.CompilerParams(vmem_limit_bytes=8 << 20),
        name="join",
    )(covs[0], *to_y(covs))
    parts, projected = lax.optimization_barrier((parts, projected))
    rings = [[y * NZ + z for z in range(NZ)] for y in range(NY)]
    parts = lax.all_to_all(parts, "dp", 0, 0, axis_index_groups=rings, tiled=True)
    covariance = pl.pallas_call(
        finish_kernel,
        out_shape=jax.ShapeDtypeStruct((2, width, width), jnp.float32),
        compiler_params=pltpu.CompilerParams(vmem_limit_bytes=8 << 20),
        name="finish",
    )(parts)
    projected = projected.reshape(2, owned, projected.shape[3], projected.shape[4])
    return (covariance.reshape(1, 2 * width * width), projected)


def solution(mesh):
    placed = (
        P(("dp", "order"), None, None),
        P(),
        P(),
        P("order"),
        P("order", None, None),
        P("order", None, None),
    )
    return jax.shard_map(
        body,
        mesh=mesh,
        in_specs=placed,
        out_specs=(P(("order", "dp"), None), P(None, "order", "dp", None)),
        check_vma=False,
    )
```
